256 devices in a mesh: lat: 16 (over x, y_hi, core), lon: 8 (over z), ch: 2 (over y_lo).
Axes of the slice: x: 4, y: 4 (y_hi: 2, y_lo: 2; y = y_hi * 2 + y_lo), z: 8, core: 2. Of those that a mesh axis runs over, the one named last changes fastest.
Arguments:
- grid_tokens: bfloat16 [1, 256, 768, 768], P(None, 'lat', 'lon'), may hold values from -6 to 6
- first_gain: float32 [768], replicated, may hold values from 0.1 to 1.9
- first_bias: float32 [768], replicated, may hold values from -3 to 3
- first_filter: bfloat16 [2, 8, 96, 96], P(None, 'ch'), may hold values from -0.4375 to 0.4375
- first_shift: float32 [2, 8, 96], P(None, 'ch'), may hold values from -3 to 3
- second_filter: bfloat16 [2, 8, 96, 96], P(None, 'ch'), may hold values from -0.4375 to 0.4375
- second_shift: float32 [2, 8, 96], P(None, 'ch'), may hold values from -3 to 3
- mode_mask: int32 [256, 384], P(None, ('lat', 'lon')), may hold values 0 or 1
- second_gain: float32 [768], replicated, may hold values from 0.1 to 1.9
- second_bias: float32 [768], replicated, may hold values from -3 to 3
- up_weight: bfloat16 [768, 3072], P(None, 'ch'), may hold values from -0.21875 to 0.21875
- up_bias: float32 [3072], P('ch'), may hold values from -3 to 3
- down_weight: bfloat16 [3072, 768], P('ch'), may hold values from -0.109375 to 0.109375
- down_bias: float32 [768], P('ch'), may hold values from -3 to 3
Outputs:
- block_output: bfloat16 [1, 256, 768, 768], P(None, ('lat', 'lon'), None, 'ch')
The draws below stay inside these ranges and needn't reach their ends.
Inputs may be any that keep to these rules, and one draw needn't show every extreme that they name: `mode_mask`: 1 keeps a mode, 0 drops it.
All inputs are finite; a program needn't handle non-finite values. No bound on the sum of `mode_mask` on one device may be relied on, other than what follows from the above.
Results may differ from the reference program's by a relative error of at most 0.009.
Values may be sent and summed in bfloat16 or wider, within the bound.
No kernel may reach another device: no remote copies, remote signals or barrier semaphores. Data moves between devices by JAX's collectives and lax.ppermute only.
A program may use at most 64 MiB of HBM per device.

```python
import math
import jax
import jax.numpy as jnp
from jax import lax

SAMPLES = 1
LAT_ROWS = 256
LON_COLS = 768
LON_MODES = 384
CHANNELS = 768
BLOCKS = 8
BLOCK_SIZE = 96
HIDDEN_SIZE = 3072
N_CH = 2


def set_ends(entries, rng, low, high):
    shape = entries.shape
    place = [jax.random.randint(jax.random.fold_in(rng, axis), (), 0, shape[axis]) for axis in range(len(shape))]
    entries = entries.at[tuple(place)].set(low)
    longest = shape.index(max(shape))
    place[longest] = (place[longest] + 1) % shape[longest]
    return entries.at[tuple(place)].set(high)


def levels(own_key, dims, shards, low, top_value):
    level = 1.0
    for axis_at, parts in shards:
        draws = jax.random.uniform(jax.random.fold_in(jax.random.fold_in(own_key, 6), axis_at), (parts,), jnp.float32, low / len(shards), top_value / len(shards))
        level = level * jnp.repeat(jnp.exp(draws), dims[axis_at] // parts).reshape((-1,) + (1,) * (len(dims) - 1 - axis_at))
    return level


def bell_draw(stream_key, shape, width, limit, pieces=(), kind=jnp.bfloat16):
    factor_of = levels(stream_key, shape, pieces, -0.22, 0.18) if pieces else 1.0
    values = jax.random.normal(stream_key, shape, jnp.float32) * width * factor_of
    return jnp.minimum(jnp.maximum(values, -limit), limit).astype(kind)


def setup_inputs(seed: int = 0) -> dict:
    key_list = jax.random.split(jax.random.key(seed), 15)
    return {
        "grid_tokens": bell_draw(key_list[0], (SAMPLES, LAT_ROWS, LON_COLS, CHANNELS), 1.0, 6.0, ((1, 16), (2, 8))),
        "first_gain": jnp.clip(1.0 + 0.18 * jax.random.normal(key_list[1], (CHANNELS,), jnp.float32), 0.1, 1.9),
        "first_bias": bell_draw(key_list[2], (CHANNELS,), 0.5, 3.0, (), jnp.float32),
        "first_filter": bell_draw(key_list[3], (2, BLOCKS, BLOCK_SIZE, BLOCK_SIZE), (2 * BLOCK_SIZE) ** -0.5, 0.4375, ((1, 2),)),
        "first_shift": bell_draw(key_list[4], (2, BLOCKS, BLOCK_SIZE), 0.5, 3.0, ((1, 2),), jnp.float32),
        "second_filter": bell_draw(key_list[5], (2, BLOCKS, BLOCK_SIZE, BLOCK_SIZE), (2 * BLOCK_SIZE) ** -0.5, 0.4375, ((1, 2),)),
        "second_shift": bell_draw(key_list[6], (2, BLOCKS, BLOCK_SIZE), 0.5, 3.0, ((1, 2),), jnp.float32),
        "mode_mask": set_ends((jax.random.randint(key_list[7], (LAT_ROWS, LON_MODES), 0, 4) < 3).astype(jnp.int32), jax.random.fold_in(key_list[7], 1), 0, 1),
        "second_gain": jnp.clip(1.0 + 0.18 * jax.random.normal(key_list[8], (CHANNELS,), jnp.float32), 0.1, 1.9),
        "second_bias": bell_draw(key_list[9], (CHANNELS,), 0.5, 3.0, (), jnp.float32),
        "up_weight": bell_draw(key_list[10], (CHANNELS, HIDDEN_SIZE), CHANNELS ** -0.5, 0.21875, ((1, 2),)),
        "up_bias": bell_draw(key_list[11], (HIDDEN_SIZE,), 0.5, 3.0, ((0, 2),), jnp.float32),
        "down_weight": bell_draw(key_list[12], (HIDDEN_SIZE, CHANNELS), HIDDEN_SIZE ** -0.5, 0.109375, ((0, 2),)),
        "down_bias": bell_draw(key_list[13], (CHANNELS,), 0.5, 3.0, ((0, 2),), jnp.float32),
    }


shrink_level = 0.01
norm_epsilon = 1e-05

def layer_norm(values, gain_vector, shift_vector):
    values = values.astype(jnp.float32)
    center = lax.optimization_barrier(jnp.mean(values, axis=-1, keepdims=True))
    spread = lax.optimization_barrier(jnp.mean(jnp.square(values - center), axis=-1, keepdims=True))
    return (values - center) * lax.rsqrt(spread + norm_epsilon) * gain_vector + shift_vector

def lon_tables(lon_width, mode_count):
    frequency = jnp.arange(mode_count, dtype=jnp.int32)[:, None]
    position = jnp.arange(lon_width, dtype=jnp.int32)[None, :]
    phases = frequency * position % lon_width
    angles = phases.astype(jnp.float32) * (2.0 * math.pi / lon_width)
    norm_scale = 1.0 / math.sqrt(lon_width)
    forward = jnp.stack([jnp.cos(angles) * norm_scale, -jnp.sin(angles) * norm_scale]).astype(jnp.bfloat16)
    factor = jnp.where(frequency == 0, 1.0, 2.0) * norm_scale
    inverse = jnp.stack([jnp.cos(angles) * factor, -jnp.sin(angles) * factor]).astype(jnp.bfloat16)
    return (forward, inverse)

def lat_tables(lat_height):
    indices = jnp.arange(lat_height, dtype=jnp.int32)
    phases = indices[:, None] * indices[None, :] % lat_height
    angles = phases.astype(jnp.float32) * (2.0 * math.pi / lat_height)
    norm_scale = 1.0 / math.sqrt(lat_height)
    cosine = jnp.cos(angles) * norm_scale
    sine_table = jnp.sin(angles) * norm_scale
    forward = jnp.stack([jnp.stack([cosine, sine_table]), jnp.stack([-sine_table, cosine])]).astype(jnp.bfloat16)
    inverse = jnp.stack([jnp.stack([cosine, -sine_table]), jnp.stack([sine_table, cosine])]).astype(jnp.bfloat16)
    return (forward, inverse)

def complex_weight(weights):
    real_part, imag_part = (weights[0], weights[1])
    top_half = jnp.stack([real_part, imag_part], axis=2)
    low_half = jnp.stack([-imag_part, real_part], axis=2)
    return jnp.stack([top_half, low_half])

def mode_mixer(spectrum, weight_one, shift_one, weight_two, shift_two, keep_mask):
    samples, _, lat_freqs, lon_freqs, channel_count = spectrum.shape
    block_count = weight_one.shape[1]
    block_width = weight_one.shape[2]
    split_spec = spectrum.reshape(samples, 2, lat_freqs, lon_freqs, block_count, block_width).astype(jnp.float32)
    first_layer = jnp.einsum('bpxyni,pniqo->bqxyno', split_spec, complex_weight(weight_one).astype(jnp.float32))
    first_layer = jnp.maximum(first_layer + shift_one[None, :, None, None, :, :], 0.0).astype(jnp.bfloat16)
    second_layer = jnp.einsum('bpxyni,pniqo->bqxyno', first_layer.astype(jnp.float32), complex_weight(weight_two).astype(jnp.float32))
    second_layer = second_layer + shift_two[None, :, None, None, :, :]
    second_layer = second_layer - jnp.clip(second_layer, -shrink_level, shrink_level)
    second_layer = second_layer * keep_mask.astype(jnp.float32)[None, None, :, :, None, None]
    return second_layer.astype(jnp.bfloat16).reshape(samples, 2, lat_freqs, lon_freqs, channel_count)

def reference(grid_tokens, first_gain, first_bias, first_filter, first_shift, second_filter, second_shift, mode_mask, second_gain, second_bias, up_weight, up_bias, down_weight, down_bias):
    normed = layer_norm(grid_tokens, first_gain, first_bias).astype(jnp.bfloat16)
    lon_forward, lon_inverse = lon_tables(LON_COLS, LON_MODES)
    lat_forward, lat_inverse = lat_tables(LAT_ROWS)
    row_spectrum = jnp.einsum('pkw,bhwc->bhpkc', lon_forward.astype(jnp.float32), normed.astype(jnp.float32)).astype(jnp.bfloat16)
    spectrum = jnp.einsum('qpxh,bhpyc->bqxyc', lat_forward.astype(jnp.float32), row_spectrum.astype(jnp.float32)).astype(jnp.bfloat16)
    filtered_modes = mode_mixer(spectrum, first_filter, first_shift, second_filter, second_shift, mode_mask)
    row_modes = jnp.einsum('qphx,bpxyc->bhqyc', lat_inverse.astype(jnp.float32), filtered_modes.astype(jnp.float32)).astype(jnp.bfloat16)
    filtered = jnp.einsum('pkw,bhpkc->bhwc', lon_inverse.astype(jnp.float32), row_modes.astype(jnp.float32))
    mixed = (grid_tokens.astype(jnp.float32) + normed.astype(jnp.float32) + filtered).astype(jnp.bfloat16)
    group_width = HIDDEN_SIZE // N_CH
    down_groups = down_weight.reshape(N_CH, group_width, CHANNELS).astype(jnp.float32)

    def feed_forward(row_slab):
        normed_two = layer_norm(row_slab, second_gain, second_bias).astype(jnp.bfloat16)
        tokens = normed_two.reshape(-1, CHANNELS)
        hidden = jnp.dot(tokens, up_weight, preferred_element_type=jnp.float32) + up_bias
        hidden = jax.nn.gelu(hidden, approximate=False).astype(jnp.bfloat16)
        grouped = hidden.reshape(-1, N_CH, group_width).astype(jnp.float32)
        partials = jnp.einsum('tgj,gjc->tgc', grouped, down_groups).astype(jnp.bfloat16)
        total_sum = lax.optimization_barrier(jnp.sum(partials.astype(jnp.float32), axis=1)) + down_bias + row_slab.reshape(-1, CHANNELS).astype(jnp.float32)
        return total_sum.astype(jnp.bfloat16).reshape(row_slab.shape)
    results = lax.map(feed_forward, jnp.swapaxes(mixed, 0, 1))
    return jnp.swapaxes(results, 0, 1)
```

```python
import math

import jax
import jax.numpy as jnp
from jax import lax
from jax.sharding import PartitionSpec as P

shrink_level = 0.01
norm_epsilon = 1e-05


def lon_tables(lon_width, mode_count):
    frequency = jnp.arange(mode_count, dtype=jnp.int32)[:, None]
    position = jnp.arange(lon_width, dtype=jnp.int32)[None, :]
    phases = frequency * position % lon_width
    angles = phases.astype(jnp.float32) * (2.0 * math.pi / lon_width)
    norm_scale = 1.0 / math.sqrt(lon_width)
    forward = jnp.stack([jnp.cos(angles) * norm_scale, -jnp.sin(angles) * norm_scale]).astype(
        jnp.bfloat16
    )
    factor = jnp.where(frequency == 0, 1.0, 2.0) * norm_scale
    inverse = jnp.stack([jnp.cos(angles) * factor, -jnp.sin(angles) * factor]).astype(jnp.bfloat16)
    return (forward, inverse)


def lat_tables(lat_height):
    indices = jnp.arange(lat_height, dtype=jnp.int32)
    phases = indices[:, None] * indices[None, :] % lat_height
    angles = phases.astype(jnp.float32) * (2.0 * math.pi / lat_height)
    norm_scale = 1.0 / math.sqrt(lat_height)
    cosine = jnp.cos(angles) * norm_scale
    sine_table = jnp.sin(angles) * norm_scale
    forward = jnp.stack([jnp.stack([cosine, sine_table]), jnp.stack([-sine_table, cosine])]).astype(
        jnp.bfloat16
    )
    inverse = jnp.stack([jnp.stack([cosine, -sine_table]), jnp.stack([sine_table, cosine])]).astype(
        jnp.bfloat16
    )
    return (forward, inverse)


def complex_weight(weights):
    real_part, imag_part = (weights[0], weights[1])
    top_half = jnp.stack([real_part, imag_part], axis=2)
    low_half = jnp.stack([-imag_part, real_part], axis=2)
    return jnp.stack([top_half, low_half])


def mode_mixer(spectrum, weight_one, shift_one, weight_two, shift_two, keep_mask):
    samples, _, lat_freqs, lon_freqs, channel_count = spectrum.shape
    block_count = weight_one.shape[1]
    block_width = weight_one.shape[2]
    split_spec = spectrum.reshape(samples, 2, lat_freqs, lon_freqs, block_count, block_width)
    first_layer = jnp.einsum(
        "bpxyni,pniqo->bqxyno",
        split_spec,
        complex_weight(weight_one),
        preferred_element_type=jnp.float32,
    )
    first_layer = jnp.maximum(first_layer + shift_one[None, :, None, None, :, :], 0.0).astype(
        jnp.bfloat16
    )
    second_layer = jnp.einsum(
        "bpxyni,pniqo->bqxyno",
        first_layer,
        complex_weight(weight_two),
        preferred_element_type=jnp.float32,
    )
    second_layer = second_layer + shift_two[None, :, None, None, :, :]
    second_layer = second_layer - jnp.clip(second_layer, -shrink_level, shrink_level)
    second_layer = second_layer * keep_mask.astype(jnp.float32)[None, None, :, :, None, None]
    return second_layer.astype(jnp.bfloat16).reshape(
        samples, 2, lat_freqs, lon_freqs, channel_count
    )


def token_norm(values, gain, bias):
    values = values.astype(jnp.float32)
    center = jnp.mean(values, axis=-1, keepdims=True)
    spread = jnp.mean(jnp.square(values - center), axis=-1, keepdims=True)
    return ((values - center) * lax.rsqrt(spread + norm_epsilon) * gain + bias).astype(jnp.bfloat16)


def other_half(up_weight, down_weight, up_bias, down_bias):
    core = lax.axis_index("lat") % 2
    swap = [(0, 1), (1, 0)]
    lat_count = lax.axis_size("lat")
    siblings = [(place, place ^ 1) for place in range(lat_count)]
    result = []
    for weight in (up_weight, down_weight):
        rows = weight.shape[0] // 2
        mine = lax.dynamic_slice_in_dim(weight, core * rows, rows, 0)
        fetched = lax.ppermute(mine, "ch", swap)
        shared = lax.ppermute(fetched, "lat", siblings)
        low = jnp.where(core == 0, fetched, shared)
        high = jnp.where(core == 0, shared, fetched)
        result.append(jnp.concatenate([low, high]))
    biases = lax.ppermute(jnp.concatenate([up_bias, down_bias]), "ch", swap)
    return (*result, biases[: up_bias.shape[0]], biases[up_bias.shape[0] :])


def shards(
    grid_tokens,
    first_gain,
    first_bias,
    first_filter,
    first_shift,
    second_filter,
    second_shift,
    mode_mask,
    second_gain,
    second_bias,
    up_weight,
    up_bias,
    down_weight,
    down_bias,
):
    lat_count = lax.axis_size("lat")
    lon_count = lax.axis_size("lon")
    ch_count = lax.axis_size("ch")
    everyone = ("lat", "lon", "ch")
    samples, rows_here, cols_here, channel_count = grid_tokens.shape
    full_width = cols_here * lon_count
    full_height = rows_here * lat_count
    part_chans = channel_count // ch_count
    mode_count = full_width // 2
    spread_count = lat_count * lon_count
    device_count = spread_count * ch_count
    modes_here = mode_count // spread_count
    ch_place = lax.axis_index("ch")
    by_row = grid_tokens.reshape(lon_count, ch_count, cols_here, channel_count)
    to_send = lax.dynamic_index_in_dim(by_row, ch_place, 1, keepdims=False)
    tokens = lax.all_to_all(to_send, "lon", split_axis=0, concat_axis=0, tiled=True)
    tokens = tokens.reshape(full_width, channel_count)
    up_other, down_other, up_bias_other, down_bias_other = other_half(
        up_weight, down_weight, up_bias, down_bias
    )
    normed = token_norm(tokens, first_gain, first_bias)
    lon_forward, lon_inverse = lon_tables(full_width, mode_count)
    lat_forward, lat_inverse = lat_tables(full_height)
    forward_rows = jnp.swapaxes(lon_forward, 0, 1).reshape(2 * mode_count, full_width)
    inverse_rows = jnp.swapaxes(lon_inverse, 0, 1).reshape(2 * mode_count, full_width)
    halves = [
        jnp.dot(
            forward_rows,
            normed[:, half * part_chans : (half + 1) * part_chans],
            preferred_element_type=jnp.float32,
        )
        .astype(jnp.bfloat16)
        .reshape(spread_count, 1, 2 * modes_here, part_chans)
        for half in range(ch_count)
    ]
    packed = jnp.concatenate(halves, 1).reshape(device_count, 2 * modes_here, part_chans)
    arrived = lax.all_to_all(packed, everyone, split_axis=0, concat_axis=0, tiled=True)
    spectrum_rows = arrived.reshape(full_height, modes_here, 2, part_chans)
    spectrum = jnp.einsum(
        "qpxh,hypc->qxyc", lat_forward, spectrum_rows, preferred_element_type=jnp.float32
    ).astype(jnp.bfloat16)[None]
    filtered_modes = mode_mixer(
        spectrum, first_filter, first_shift, second_filter, second_shift, mode_mask
    )[0]
    back_rows = jnp.einsum(
        "qphx,pxyc->hyqc", lat_inverse, filtered_modes, preferred_element_type=jnp.float32
    ).astype(jnp.bfloat16)
    packed_back = back_rows.reshape(device_count, 2 * modes_here, part_chans)
    returned = lax.all_to_all(packed_back, everyone, split_axis=0, concat_axis=0, tiled=True)
    returned = returned.reshape(spread_count, ch_count, 2 * modes_here, part_chans)
    filtered = jnp.concatenate(
        [
            jnp.einsum(
                "mw,mc->wc",
                inverse_rows,
                returned[:, half].reshape(2 * mode_count, part_chans),
                preferred_element_type=jnp.float32,
            )
            for half in range(ch_count)
        ],
        axis=1,
    )
    mixed = (tokens.astype(jnp.float32) + normed.astype(jnp.float32) + filtered).astype(jnp.bfloat16)
    normed_two = token_norm(mixed, second_gain, second_bias)
    total = mixed.astype(jnp.float32)
    bias_low = jnp.where(ch_place == 0, down_bias, down_bias_other)
    bias_high = jnp.where(ch_place == 0, down_bias_other, down_bias)
    total = total + jnp.concatenate([bias_low, bias_high])
    for up, up_shift, down in (
        (up_weight, up_bias, down_weight),
        (up_other, up_bias_other, down_other),
    ):
        hidden = jnp.dot(normed_two, up, preferred_element_type=jnp.float32) + up_shift
        hidden = jax.nn.gelu(hidden, approximate=False).astype(jnp.bfloat16)
        partial = jnp.dot(hidden, down, preferred_element_type=jnp.float32).astype(jnp.bfloat16)
        total = total + partial.astype(jnp.float32)
    result = total.astype(jnp.bfloat16)
    split = jnp.stack([result[:, :part_chans], result[:, part_chans:]])
    swapped = lax.all_to_all(split, "ch", split_axis=0, concat_axis=0, tiled=True)
    return swapped.reshape(samples, ch_count, full_width, part_chans)


def solution(mesh):
    in_specs = (
        P(None, "lat", "lon", None),
        P(),
        P(),
        P(None, "ch", None, None),
        P(None, "ch", None),
        P(None, "ch", None, None),
        P(None, "ch", None),
        P(None, ("lat", "lon")),
        P(),
        P(),
        P(None, "ch"),
        P("ch"),
        P("ch", None),
        P("ch"),
    )
    out_specs = P(None, ("lat", "lon"), None, "ch")
    return jax.shard_map(shards, mesh=mesh, in_specs=in_specs, out_specs=out_specs, check_vma=False)
```

```python
import math

import jax
import jax.numpy as jnp
from jax import lax
from jax.sharding import PartitionSpec as P

shrink_level = 0.01
norm_epsilon = 1e-05


def lon_table(lon_width, mode_count):
    frequency = jnp.arange(mode_count, dtype=jnp.int32)[:, None]
    position = jnp.arange(lon_width, dtype=jnp.int32)[None, :]
    phases = frequency * position % lon_width
    angles = phases.astype(jnp.float32) * (2.0 * math.pi / lon_width)
    norm_scale = 1.0 / math.sqrt(lon_width)
    return jnp.stack([jnp.cos(angles) * norm_scale, -jnp.sin(angles) * norm_scale]).astype(jnp.bfloat16)


def lat_tables(lat_height):
    indices = jnp.arange(lat_height, dtype=jnp.int32)
    phases = indices[:, None] * indices[None, :] % lat_height
    angles = phases.astype(jnp.float32) * (2.0 * math.pi / lat_height)
    norm_scale = 1.0 / math.sqrt(lat_height)
    cosine = jnp.cos(angles) * norm_scale
    sine_table = jnp.sin(angles) * norm_scale
    forward = jnp.stack([jnp.stack([cosine, sine_table]), jnp.stack([-sine_table, cosine])]).astype(
        jnp.bfloat16
    )
    inverse = jnp.stack([jnp.stack([cosine, -sine_table]), jnp.stack([sine_table, cosine])]).astype(
        jnp.bfloat16
    )
    return (forward, inverse)


def complex_weight(weights):
    real_part, imag_part = (weights[0], weights[1])
    top_half = jnp.stack([real_part, imag_part], axis=2)
    low_half = jnp.stack([-imag_part, real_part], axis=2)
    return jnp.stack([top_half, low_half])


def mode_mixer(spectrum, weight_one, shift_one, weight_two, shift_two, keep_mask):
    samples, _, lat_freqs, lon_freqs, channel_count = spectrum.shape
    block_count = weight_one.shape[1]
    block_width = weight_one.shape[2]
    split_spec = spectrum.reshape(samples, 2, lat_freqs, lon_freqs, block_count, block_width)
    first_layer = jnp.einsum(
        "bpxyni,pniqo->bqxyno",
        split_spec,
        complex_weight(weight_one),
        preferred_element_type=jnp.float32,
    )
    first_layer = jnp.maximum(first_layer + shift_one[None, :, None, None, :, :], 0.0).astype(
        jnp.bfloat16
    )
    second_layer = jnp.einsum(
        "bpxyni,pniqo->bqxyno",
        first_layer,
        complex_weight(weight_two),
        preferred_element_type=jnp.float32,
    )
    second_layer = second_layer + shift_two[None, :, None, None, :, :]
    second_layer = second_layer - jnp.clip(second_layer, -shrink_level, shrink_level)
    second_layer = second_layer * keep_mask.astype(jnp.float32)[None, None, :, :, None, None]
    return second_layer.astype(jnp.bfloat16).reshape(
        samples, 2, lat_freqs, lon_freqs, channel_count
    )


def token_norm(values, gain, bias):
    values = values.astype(jnp.float32)
    center = jnp.mean(values, axis=-1, keepdims=True)
    spread = jnp.mean(jnp.square(values - center), axis=-1, keepdims=True)
    return ((values - center) * lax.rsqrt(spread + norm_epsilon) * gain + bias).astype(jnp.bfloat16)


def fetch_half(weight, core):
    rows = weight.shape[0] // 2
    mine = lax.dynamic_slice_in_dim(weight, core * rows, rows, 0)
    return lax.ppermute(mine, "ch", [(0, 1), (1, 0)])


def join_halves(fetched, core):
    siblings = [(place, place ^ 1) for place in range(lax.axis_size("lat"))]
    shared = lax.ppermute(fetched, "lat", siblings)
    low = jnp.where(core == 0, fetched, shared)
    high = jnp.where(core == 0, shared, fetched)
    return jnp.concatenate([low, high])


def shards(
    grid_tokens,
    first_gain,
    first_bias,
    first_filter,
    first_shift,
    second_filter,
    second_shift,
    mode_mask,
    second_gain,
    second_bias,
    up_weight,
    up_bias,
    down_weight,
    down_bias,
):
    lat_count = lax.axis_size("lat")
    lon_count = lax.axis_size("lon")
    ch_count = lax.axis_size("ch")
    everyone = ("lat", "lon", "ch")
    samples, rows_here, cols_here, channel_count = grid_tokens.shape
    full_width = cols_here * lon_count
    full_height = rows_here * lat_count
    part_chans = channel_count // ch_count
    mode_count = full_width // 2
    spread_count = lat_count * lon_count
    device_count = spread_count * ch_count
    modes_here = mode_count // spread_count
    ch_place = lax.axis_index("ch")
    by_row = grid_tokens.reshape(lon_count, ch_count, cols_here, channel_count)
    to_send = lax.dynamic_index_in_dim(by_row, ch_place, 1, keepdims=False)
    tokens = lax.all_to_all(to_send, "lon", split_axis=0, concat_axis=0, tiled=True)
    tokens = tokens.reshape(full_width, channel_count)
    core = lax.axis_index("lat") % 2
    up_fetched = fetch_half(up_weight, core)
    biases = lax.ppermute(jnp.concatenate([up_bias, down_bias]), "ch", [(0, 1), (1, 0)])
    hidden_here = up_bias.shape[0]
    up_bias_other, down_bias_other = biases[:hidden_here], biases[hidden_here:]
    normed = token_norm(tokens, first_gain, first_bias)
    lon_forward = lon_table(full_width, mode_count)
    lat_forward, lat_inverse = lat_tables(full_height)
    forward_rows = jnp.swapaxes(lon_forward, 0, 1).reshape(2 * mode_count, full_width)
    halves = [
        jnp.dot(
            forward_rows,
            normed[:, half * part_chans : (half + 1) * part_chans],
            preferred_element_type=jnp.float32,
        )
        .astype(jnp.bfloat16)
        .reshape(spread_count, 1, 2 * modes_here, part_chans)
        for half in range(ch_count)
    ]
    packed = jnp.concatenate(halves, 1).reshape(device_count, 2 * modes_here, part_chans)
    packed, up_fetched = lax.optimization_barrier((packed, up_fetched))
    down_fetched = fetch_half(lax.optimization_barrier((down_weight, up_fetched))[0], core)
    up_other = join_halves(up_fetched, core)
    arrived = lax.all_to_all(packed, everyone, split_axis=0, concat_axis=0, tiled=True)
    spectrum_rows = arrived.reshape(full_height, modes_here, 2, part_chans)
    spectrum = jnp.einsum(
        "qpxh,hypc->qxyc", lat_forward, spectrum_rows, preferred_element_type=jnp.float32
    ).astype(jnp.bfloat16)[None]
    filtered_modes = mode_mixer(
        spectrum, first_filter, first_shift, second_filter, second_shift, mode_mask
    )[0]
    first_mode = (lax.axis_index("lat") * lon_count + lax.axis_index("lon")) * modes_here
    factor = jnp.where(first_mode + jnp.arange(modes_here) == 0, 1.0, 2.0)[None, :, None, None]
    back_rows = jnp.einsum(
        "qphx,pxyc->hyqc", lat_inverse, filtered_modes, preferred_element_type=jnp.float32
    )
    back_rows = (back_rows * factor).astype(jnp.bfloat16)
    packed_back = back_rows.reshape(device_count, 2 * modes_here, part_chans)
    packed_back, down_fetched = lax.optimization_barrier((packed_back, down_fetched))
    down_other = join_halves(down_fetched, core)
    returned = lax.all_to_all(packed_back, everyone, split_axis=0, concat_axis=0, tiled=True)
    returned = returned.reshape(spread_count, ch_count, 2 * modes_here, part_chans)
    filtered = jnp.concatenate(
        [
            jnp.einsum(
                "mw,mc->wc",
                forward_rows,
                returned[:, half].reshape(2 * mode_count, part_chans),
                preferred_element_type=jnp.float32,
            )
            for half in range(ch_count)
        ],
        axis=1,
    )
    mixed = (tokens.astype(jnp.float32) + normed.astype(jnp.float32) + filtered).astype(jnp.bfloat16)
    bias_low = jnp.where(ch_place == 0, down_bias, down_bias_other)
    bias_high = jnp.where(ch_place == 0, down_bias_other, down_bias)
    down_shift = jnp.concatenate([bias_low, bias_high])
    kept, received = [], []
    chunk = full_width // 2
    for start in range(0, full_width, chunk):
        piece = mixed[start : start + chunk]
        if kept:
            piece, kept[-1] = lax.optimization_barrier((piece, kept[-1]))
        normed_two = token_norm(piece, second_gain, second_bias)
        total = piece.astype(jnp.float32) + down_shift
        for up, up_shift, down in (
            (up_weight, up_bias, down_weight),
            (up_other, up_bias_other, down_other),
        ):
            hidden = jnp.dot(normed_two, up, preferred_element_type=jnp.float32) + up_shift
            hidden = jax.nn.gelu(hidden, approximate=False).astype(jnp.bfloat16)
            partial = jnp.dot(hidden, down, preferred_element_type=jnp.float32).astype(jnp.bfloat16)
            total = total + partial.astype(jnp.float32)
        result = total.astype(jnp.bfloat16)
        low, high = result[:, :part_chans], result[:, part_chans:]
        kept.append(jnp.where(ch_place == 0, low, high))
        given = jnp.where(ch_place == 0, high, low)
        received.append(lax.ppermute(given, "ch", [(0, 1), (1, 0)]))
    kept, received = jnp.concatenate(kept), jnp.concatenate(received)
    even = jnp.where(ch_place == 0, kept, received)
    odd = jnp.where(ch_place == 0, received, kept)
    return jnp.stack([even, odd])[None]


def solution(mesh):
    in_specs = (
        P(None, "lat", "lon", None),
        P(),
        P(),
        P(None, "ch", None, None),
        P(None, "ch", None),
        P(None, "ch", None, None),
        P(None, "ch", None),
        P(None, ("lat", "lon")),
        P(),
        P(),
        P(None, "ch"),
        P("ch"),
        P("ch", None),
        P("ch"),
    )
    out_specs = P(None, ("lat", "lon"), None, "ch")
    return jax.shard_map(shards, mesh=mesh, in_specs=in_specs, out_specs=out_specs, check_vma=False)
```

```python
import math

import jax
import jax.numpy as jnp
from jax import lax
from jax.experimental import pallas as pl
from jax.experimental.pallas import tpu as pltpu
from jax.sharding import PartitionSpec as P

shrink_level = 0.01
norm_epsilon = 1e-05
LANES = 128


def lon_table(lon_width, mode_count):
    frequency = jnp.arange(mode_count, dtype=jnp.int32)[:, None]
    position = jnp.arange(lon_width, dtype=jnp.int32)[None, :]
    phases = frequency * position % lon_width
    angles = phases.astype(jnp.float32) * (2.0 * math.pi / lon_width)
    norm_scale = 1.0 / math.sqrt(lon_width)
    return jnp.stack([jnp.cos(angles) * norm_scale, -jnp.sin(angles) * norm_scale]).astype(jnp.bfloat16)


def token_norm(values, gain, bias):
    values = values.astype(jnp.float32)
    center = jnp.mean(values, axis=-1, keepdims=True)
    spread = jnp.mean(jnp.square(values - center), axis=-1, keepdims=True)
    return ((values - center) * lax.rsqrt(spread + norm_epsilon) * gain + bias).astype(jnp.bfloat16)


def lat_table(lat_height, row_order):
    frequency = jnp.arange(lat_height, dtype=jnp.int32)[:, None]
    phases = frequency * row_order[None, :] % lat_height
    angles = phases.astype(jnp.float32) * (2.0 * math.pi / lat_height)
    norm_scale = 1.0 / math.sqrt(lat_height)
    cosine = jnp.cos(angles) * norm_scale
    sine_table = jnp.sin(angles) * norm_scale
    forward = jnp.stack([jnp.stack([cosine, sine_table]), jnp.stack([-sine_table, cosine])]).astype(
        jnp.bfloat16
    )
    split = forward.reshape(2, 2, lat_height, 8, lat_height // 8)
    return split.transpose(0, 2, 3, 1, 4).reshape(2 * lat_height, 2 * lat_height)


def filter_matrix(weights):
    block = weights.shape[-1]
    room = LANES - block
    real_part, imag_part = (jnp.pad(part, ((0, room), (0, room))) for part in (weights[0], weights[1]))
    return jnp.concatenate(
        [
            jnp.concatenate([real_part, imag_part], 1),
            jnp.concatenate([-imag_part, real_part], 1),
        ]
    )


def pack_kernel(tokens_ref, mask_ref, even_ref, odd_ref):
    parts, block = 8, 96
    lane = lax.broadcasted_iota(jnp.int32, (block, LANES), 1)
    for turn, out_ref in enumerate((even_ref, odd_ref)):
        rows = [tokens_ref[2 * group + turn] for group in range(4)]
        stats = jnp.zeros((block, LANES), jnp.float32)
        for group, row in enumerate(rows):
            values = row.astype(jnp.float32)
            center = jnp.mean(values, axis=-1, keepdims=True)
            spread = jnp.mean(jnp.square(values - center), axis=-1, keepdims=True)
            stats = jnp.where(lane == group, center, stats)
            stats = jnp.where(lane == 4 + group, lax.rsqrt(spread + norm_epsilon), stats)
        stats = jnp.concatenate([stats, jnp.zeros((LANES - block, LANES), jnp.float32)])
        stats = jnp.transpose(stats)[:8]
        high = stats.astype(jnp.bfloat16)
        rest = stats - high.astype(jnp.float32)
        middle = rest.astype(jnp.bfloat16)
        low = (rest - middle.astype(jnp.float32)).astype(jnp.bfloat16)
        tail = jnp.concatenate(
            [
                jnp.concatenate([high, middle, low], 1).astype(jnp.float32),
                mask_ref[...],
            ]
        ).astype(jnp.bfloat16)
        for part in range(parts):
            out_ref[part, :block] = jnp.concatenate(
                [row[:, part * block : (part + 1) * block] for row in rows], 1
            )
            out_ref[part, block:] = tail


def forward_kernel(arrived_ref, gain_ref, bias_ref, table_ref, normed_ref, spectrum_ref):
    block = 96
    lane = lax.broadcasted_iota(jnp.int32, (block, 4 * block), 1)

    def spread_out(columns, first):
        result = columns[:, first : first + 1]
        for group in range(1, 4):
            result = jnp.where(
                lane < group * block, result, columns[:, first + group : first + group + 1]
            )
        return result

    for source in range(8):
        tail = arrived_ref[source, block : block + 16].astype(jnp.float32)[:8]
        stats = tail[:, :LANES] + tail[:, LANES : 2 * LANES] + tail[:, 2 * LANES :]
        stats = jnp.concatenate([stats, jnp.zeros((LANES - 8, LANES), jnp.float32)])
        columns = jnp.transpose(stats)[:block]
        values = arrived_ref[source, :block].astype(jnp.float32)
        values = (values - spread_out(columns, 0)) * spread_out(columns, 4)
        values = values * gain_ref[...] + bias_ref[...]
        normed_ref[source * block : (source + 1) * block] = values.astype(jnp.bfloat16)
    spectrum_ref[...] = jnp.dot(
        table_ref[...], normed_ref[...], preferred_element_type=jnp.float32
    ).astype(jnp.bfloat16)


def modes_kernel(
    even_ref,
    odd_ref,
    forward_ref,
    inverse_ref,
    first_ref,
    first_shift_ref,
    second_ref,
    second_shift_ref,
    mask_ref,
    factor_ref,
    even_out,
    odd_out,
    in_rows,
    out_rows,
):
    sources, step, wide = 32, 24, 384
    for turn, ref in enumerate((even_ref, odd_ref)):
        for tile in range(3):
            in_rows[3 * turn + tile] = ref[:, tile * LANES : (tile + 1) * LANES].astype(jnp.float32)
    for pair in range(6):
        gathered = []
        for mode in (2 * pair, 2 * pair + 1):
            pieces = []
            loaded = [
                jnp.concatenate(
                    [
                        in_rows.at[3 * turn + tile][pl.ds(2 * mode + part, sources, stride=step), :]
                        for tile in range(3)
                    ],
                    1,
                )
                for turn in range(2)
                for part in range(2)
            ]
            for group in range(4):
                for value in loaded:
                    if group:
                        value = pltpu.roll(value, wide - 96 * group, 1)
                    pieces.append(value[:, :LANES])
            gathered.append(jnp.concatenate(pieces).astype(jnp.bfloat16))
        spectrum = jnp.dot(
            forward_ref[...], jnp.concatenate(gathered, 1), preferred_element_type=jnp.float32
        ).astype(jnp.bfloat16)
        half = spectrum.shape[0] // 2
        filtered = []
        for side in range(2):
            mode = 2 * pair + side
            lanes = slice(side * LANES, (side + 1) * LANES)
            both = jnp.concatenate([spectrum[:half, lanes], spectrum[half:, lanes]], 1)
            layer = jnp.dot(both, first_ref[...], preferred_element_type=jnp.float32)
            layer = jnp.maximum(layer + first_shift_ref[...], 0.0).astype(jnp.bfloat16)
            layer = jnp.dot(layer, second_ref[...], preferred_element_type=jnp.float32)
            layer = layer + second_shift_ref[...]
            layer = layer - jnp.clip(layer, -shrink_level, shrink_level)
            layer = (layer * mask_ref[:, mode : mode + 1]).astype(jnp.bfloat16)
            filtered.append(jnp.concatenate([layer[:, :LANES], layer[:, LANES:]]))
        back = jnp.dot(
            inverse_ref[...], jnp.concatenate(filtered, 1), preferred_element_type=jnp.float32
        )
        for side in range(2):
            mode = 2 * pair + side
            for turn in range(2):
                for part in range(2):
                    total = None
                    for group in range(4):
                        first = ((group * 2 + turn) * 2 + part) * sources
                        piece = back[first : first + sources, side * LANES : (side + 1) * LANES]
                        piece = jnp.concatenate(
                            [piece, jnp.zeros((sources, wide - LANES), jnp.float32)], 1
                        )
                        if group:
                            piece = pltpu.roll(piece, 96 * group, 1)
                        total = piece if total is None else total + piece
                    total = total * factor_ref[mode]
                    for tile in range(3):
                        out_rows.at[3 * turn + tile][
                            pl.ds(2 * mode + part, sources, stride=step), :
                        ] = total[:, tile * LANES : (tile + 1) * LANES]
    for turn, ref in enumerate((even_out, odd_out)):
        for tile in range(3):
            ref[:, tile * LANES : (tile + 1) * LANES] = out_rows[3 * turn + tile].astype(jnp.bfloat16)


def inverse_kernel(
    even_modes, odd_modes, even_ref, odd_ref, even_normed, odd_normed, table_ref, out_ref, mixed_ref
):
    block, rows = 96, 192
    for turn, (modes, tokens, normed) in enumerate(
        ((even_modes, even_ref, even_normed), (odd_modes, odd_ref, odd_normed))
    ):
        mixed = jnp.dot(table_ref[...], modes[...], preferred_element_type=jnp.float32)
        for source in range(8):
            place = slice(source * block, (source + 1) * block)
            mixed_ref[place] = (
                tokens[source, :block].astype(jnp.float32)
                + normed[place].astype(jnp.float32)
                + mixed[place]
            ).astype(jnp.bfloat16)
        for group in range(4):
            out_ref[2 * group + turn] = jnp.concatenate(
                [
                    mixed_ref[part * rows : (part + 1) * rows, group * block : (group + 1) * block]
                    for part in range(4)
                ],
                1,
            )


def unpack_kernel(arrived_ref, out_ref):
    block, rows = 96, 192
    for part in range(4):
        out_ref[part * rows : (part + 1) * rows] = jnp.concatenate(
            [arrived_ref[source, :, part * block : (part + 1) * block] for source in range(8)], 1
        )


def local_call(body, outs, *operands, scratch=(), scalars=0, flops=0):
    specs = [pl.BlockSpec(memory_space=pltpu.VMEM)] * (len(operands) - scalars)
    specs += [pl.BlockSpec(memory_space=pltpu.SMEM)] * scalars
    moved = sum(item.size * item.dtype.itemsize for item in operands)
    return pl.pallas_call(
        body,
        out_shape=outs,
        in_specs=specs,
        out_specs=jax.tree.map(lambda _: pl.BlockSpec(memory_space=pltpu.VMEM), outs),
        scratch_shapes=list(scratch),
        cost_estimate=pl.CostEstimate(flops=flops, bytes_accessed=moved, transcendentals=0),
    )(*operands)


def fetch_half(weight, core):
    rows = weight.shape[0] // 2
    mine = lax.dynamic_slice_in_dim(weight, core * rows, rows, 0)
    return lax.ppermute(mine, "ch", [(0, 1), (1, 0)])


def join_halves(fetched, core):
    siblings = [(place, place ^ 1) for place in range(lax.axis_size("lat"))]
    shared = lax.ppermute(fetched, "lat", siblings)
    low = jnp.where(core == 0, fetched, shared)
    high = jnp.where(core == 0, shared, fetched)
    return jnp.concatenate([low, high])


def shards(
    grid_tokens,
    first_gain,
    first_bias,
    first_filter,
    first_shift,
    second_filter,
    second_shift,
    mode_mask,
    second_gain,
    second_bias,
    up_weight,
    up_bias,
    down_weight,
    down_bias,
):
    lat_count = lax.axis_size("lat")
    lon_count = lax.axis_size("lon")
    ch_count = lax.axis_size("ch")
    samples, rows_here, cols_here, channel_count = grid_tokens.shape
    full_width = cols_here * lon_count
    full_height = rows_here * lat_count
    part_chans = channel_count // ch_count
    mode_count = full_width // 2
    spread_count = lat_count * lon_count
    modes_here = mode_count // spread_count
    ch_place = lax.axis_index("ch")
    lat_place, lon_place = lax.axis_index("lat"), lax.axis_index("lon")
    core = lat_place % 2
    bf16 = jnp.bfloat16
    block = channel_count // lon_count
    wide = 4 * block
    plane = ("lat", "ch")
    plane_count = lat_count * ch_count
    plane_modes = mode_count // plane_count
    swap = [(0, 1), (1, 0)]

    by_row = grid_tokens.reshape(lon_count, ch_count, cols_here, channel_count)
    row_tokens = lax.dynamic_index_in_dim(by_row, ch_place, 1, keepdims=False)
    mask_rows = jnp.pad(
        mode_mask.T.astype(jnp.float32), ((0, 8 - modes_here), (0, wide - full_height))
    )
    send_shape = jax.ShapeDtypeStruct((lon_count, cols_here + 16, wide), bf16)
    even_send, odd_send = local_call(pack_kernel, (send_shape, send_shape), row_tokens, mask_rows)
    even_tokens = lax.all_to_all(even_send, "lon", split_axis=0, concat_axis=0, tiled=True)
    odd_tokens = lax.all_to_all(odd_send, "lon", split_axis=0, concat_axis=0, tiled=True)

    up_fetched = fetch_half(up_weight, core)
    biases = lax.ppermute(jnp.concatenate([up_bias, down_bias]), "ch", swap)
    hidden_here = up_bias.shape[0]
    up_bias_other, down_bias_other = biases[:hidden_here], biases[hidden_here:]
    blocks_here = first_filter.shape[1]
    owner = lon_place // blocks_here == ch_place
    at = lon_place % blocks_here

    def block_of(array):
        own = lax.dynamic_index_in_dim(array, at, 2, keepdims=False)
        return jnp.where(owner, own, lax.ppermute(own, "ch", swap))

    filters = block_of(jnp.stack([first_filter, second_filter]))
    shifts = block_of(jnp.stack([first_shift, second_shift]))
    shifts = jnp.pad(shifts, ((0, 0), (0, 0), (0, LANES - block))).reshape(2, 1, 2 * LANES)

    lon_forward = lon_table(full_width, mode_count)
    forward_rows = jnp.swapaxes(lon_forward, 0, 1).reshape(2 * mode_count, full_width)
    inverse_rows = forward_rows.T
    group, turn, source = jnp.meshgrid(
        jnp.arange(4), jnp.arange(2), jnp.arange(plane_count), indexing="ij"
    )
    row_order = rows_here * (source // ch_count) + ch_count * (2 * group + turn) + source % ch_count
    lat_forward = lat_table(full_height, row_order.reshape(-1).astype(jnp.int32))
    lat_inverse = lat_forward.T

    gain = lax.dynamic_slice_in_dim(first_gain, lon_place * block, block, 0)
    bias = lax.dynamic_slice_in_dim(first_bias, lon_place * block, block, 0)
    gain, bias = jnp.tile(gain, 4)[None], jnp.tile(bias, 4)[None]
    row_shape = jax.ShapeDtypeStruct((full_width, wide), bf16)

    def forward(tokens):
        normed, spectrum = local_call(
            forward_kernel,
            (row_shape, row_shape),
            tokens,
            gain,
            bias,
            forward_rows,
            flops=2 * full_width * full_width * wide,
        )
        return normed, spectrum.reshape(plane_count, 2 * plane_modes, wide)

    def over_plane(array):
        moved = lax.all_to_all(
            array.reshape(plane_count, 2 * plane_modes, wide),
            plane,
            split_axis=0,
            concat_axis=0,
            tiled=True,
        )
        return moved.reshape(full_width, wide)

    even_normed, even_spectrum = forward(even_tokens)
    even_arrived = over_plane(even_spectrum)
    odd_normed, odd_spectrum = forward(odd_tokens)
    odd_spectrum, up_fetched = lax.optimization_barrier((odd_spectrum, up_fetched))
    odd_arrived = over_plane(odd_spectrum)
    down_fetched = fetch_half(lax.optimization_barrier((down_weight, up_fetched))[0], core)
    up_other = join_halves(up_fetched, core)

    masks = even_tokens[:, cols_here + 8 : cols_here + 8 + modes_here, :full_height]
    mine = lax.dynamic_slice_in_dim(masks, ch_place * (lon_count // 2), lon_count // 2, 0)
    mask = mine.reshape(plane_modes, full_height).T.astype(jnp.float32)
    first_mode = (lat_place * ch_count + ch_place) * plane_modes
    factor = jnp.where(first_mode + jnp.arange(plane_modes) == 0, 1.0, 2.0)
    row_scratch = pltpu.VMEM((6, full_width, LANES), jnp.float32)
    even_back, odd_back = local_call(
        modes_kernel,
        (row_shape, row_shape),
        even_arrived,
        odd_arrived,
        lat_forward,
        lat_inverse,
        filter_matrix(filters[0]),
        shifts[0],
        filter_matrix(filters[1]),
        shifts[1],
        mask,
        factor,
        scratch=[row_scratch] * 2,
        scalars=1,
        flops=4 * full_width * full_width * wide,
    )
    even_modes = over_plane(even_back)
    odd_modes = over_plane(odd_back)
    packed = local_call(
        inverse_kernel,
        jax.ShapeDtypeStruct((lon_count, full_width // 4, wide), bf16),
        even_modes,
        odd_modes,
        even_tokens,
        odd_tokens,
        even_normed,
        odd_normed,
        inverse_rows,
        scratch=[pltpu.VMEM((full_width, wide), bf16)],
        flops=4 * full_width * full_width * wide,
    )
    packed, down_fetched = lax.optimization_barrier((packed, down_fetched))
    down_other = join_halves(down_fetched, core)
    row = lax.all_to_all(packed, "lon", split_axis=0, concat_axis=0, tiled=True)
    mixed = local_call(
        unpack_kernel, jax.ShapeDtypeStruct((full_width, channel_count), bf16), row
    )
    bias_low = jnp.where(ch_place == 0, down_bias, down_bias_other)
    bias_high = jnp.where(ch_place == 0, down_bias_other, down_bias)
    down_shift = jnp.concatenate([bias_low, bias_high])
    normed_two = token_norm(mixed, second_gain, second_bias)
    total = mixed.astype(jnp.float32) + down_shift
    for up, up_shift, down in (
        (up_weight, up_bias, down_weight),
        (up_other, up_bias_other, down_other),
    ):
        hidden = jnp.dot(normed_two, up, preferred_element_type=jnp.float32) + up_shift
        hidden = jax.nn.gelu(hidden, approximate=False).astype(bf16)
        partial = jnp.dot(hidden, down, preferred_element_type=jnp.float32).astype(bf16)
        total = total + partial.astype(jnp.float32)
    result = total.astype(bf16)
    low, high = result[:, :part_chans], result[:, part_chans:]
    kept = jnp.where(ch_place == 0, low, high)
    given = jnp.where(ch_place == 0, high, low)
    received = lax.ppermute(given, "ch", swap)
    even = jnp.where(ch_place == 0, kept, received)
    odd = jnp.where(ch_place == 0, received, kept)
    return jnp.stack([even, odd])[None]


def solution(mesh):
    in_specs = (
        P(None, "lat", "lon", None),
        P(),
        P(),
        P(None, "ch", None, None),
        P(None, "ch", None),
        P(None, "ch", None, None),
        P(None, "ch", None),
        P(None, ("lat", "lon")),
        P(),
        P(),
        P(None, "ch"),
        P("ch"),
        P("ch", None),
        P("ch"),
    )
    out_specs = P(None, ("lat", "lon"), None, "ch")
    return jax.shard_map(shards, mesh=mesh, in_specs=in_specs, out_specs=out_specs, check_vma=False)
```

```python
import math

import jax
import jax.numpy as jnp
from jax import lax
from jax.experimental import pallas as pl
from jax.experimental.pallas import tpu as pltpu
from jax.sharding import PartitionSpec as P

shrink_level = 0.01
norm_epsilon = 1e-05
LANES = 128


def lon_table(lon_width, mode_count):
    frequency = jnp.arange(mode_count, dtype=jnp.int32)[:, None]
    position = jnp.arange(lon_width, dtype=jnp.int32)[None, :]
    phases = frequency * position % lon_width
    angles = phases.astype(jnp.float32) * (2.0 * math.pi / lon_width)
    norm_scale = 1.0 / math.sqrt(lon_width)
    return jnp.stack([jnp.cos(angles) * norm_scale, -jnp.sin(angles) * norm_scale]).astype(jnp.bfloat16)


def lat_table(lat_height, row_order):
    frequency = jnp.arange(lat_height, dtype=jnp.int32)[:, None]
    phases = frequency * row_order[None, :] % lat_height
    angles = phases.astype(jnp.float32) * (2.0 * math.pi / lat_height)
    norm_scale = 1.0 / math.sqrt(lat_height)
    cosine = jnp.cos(angles) * norm_scale
    sine_table = jnp.sin(angles) * norm_scale
    forward = jnp.stack([jnp.stack([cosine, sine_table]), jnp.stack([-sine_table, cosine])]).astype(
        jnp.bfloat16
    )
    split = forward.reshape(2, 2, lat_height, 8, lat_height // 8)
    return split.transpose(0, 2, 3, 1, 4).reshape(2 * lat_height, 2 * lat_height)


def filter_matrix(weights):
    block = weights.shape[-1]
    room = LANES - block
    real_part, imag_part = (jnp.pad(part, ((0, room), (0, room))) for part in (weights[0], weights[1]))
    return jnp.concatenate(
        [
            jnp.concatenate([real_part, imag_part], 1),
            jnp.concatenate([-imag_part, real_part], 1),
        ]
    )


def pack_kernel(tokens_ref, mask_ref, out_ref):
    parts, block = 8, 96
    lane = lax.broadcasted_iota(jnp.int32, (block, LANES), 1)
    for turn in range(2):
        rows = [tokens_ref[2 * group + turn] for group in range(4)]
        stats = jnp.zeros((block, LANES), jnp.float32)
        for group, row in enumerate(rows):
            values = row.astype(jnp.float32)
            center = jnp.mean(values, axis=-1, keepdims=True)
            spread = jnp.mean(jnp.square(values - center), axis=-1, keepdims=True)
            stats = jnp.where(lane == group, center, stats)
            stats = jnp.where(lane == 4 + group, lax.rsqrt(spread + norm_epsilon), stats)
        stats = jnp.concatenate([stats, jnp.zeros((LANES - block, LANES), jnp.float32)])
        stats = jnp.transpose(stats)[:8]
        high = stats.astype(jnp.bfloat16)
        rest = stats - high.astype(jnp.float32)
        middle = rest.astype(jnp.bfloat16)
        low = (rest - middle.astype(jnp.float32)).astype(jnp.bfloat16)
        tail = jnp.concatenate(
            [
                jnp.concatenate([high, middle, low], 1).astype(jnp.float32),
                mask_ref[...],
            ]
        ).astype(jnp.bfloat16)
        for part in range(parts):
            out_ref[part, turn, :block] = jnp.concatenate(
                [row[:, part * block : (part + 1) * block] for row in rows], 1
            )
            out_ref[part, turn, block:] = tail


def forward_kernel(arrived_ref, gain_ref, bias_ref, table_ref, normed_ref, spectrum_ref):
    block = 96
    lane = lax.broadcasted_iota(jnp.int32, (block, 4 * block), 1)

    def spread_out(columns, first):
        result = columns[:, first : first + 1]
        for group in range(1, 4):
            result = jnp.where(
                lane < group * block, result, columns[:, first + group : first + group + 1]
            )
        return result

    wide = 4 * block
    for turn in range(2):
        for source in range(8):
            tail = arrived_ref[source, turn, block : block + 16].astype(jnp.float32)[:8]
            stats = tail[:, :LANES] + tail[:, LANES : 2 * LANES] + tail[:, 2 * LANES :]
            stats = jnp.concatenate([stats, jnp.zeros((LANES - 8, LANES), jnp.float32)])
            columns = jnp.transpose(stats)[:block]
            values = arrived_ref[source, turn, :block].astype(jnp.float32)
            values = (values - spread_out(columns, 0)) * spread_out(columns, 4)
            values = values * gain_ref[...] + bias_ref[...]
            place = slice(source * block, (source + 1) * block)
            normed_ref[place, turn * wide : (turn + 1) * wide] = values.astype(jnp.bfloat16)
    spectrum_ref[...] = jnp.dot(
        table_ref[...], normed_ref[...], preferred_element_type=jnp.float32
    ).astype(jnp.bfloat16)


def modes_kernel(
    arrived_ref,
    forward_ref,
    inverse_ref,
    first_ref,
    first_shift_ref,
    second_ref,
    second_shift_ref,
    mask_ref,
    factor_ref,
    out_ref,
    in_rows,
    out_rows,
):
    sources, step, wide = 32, 24, 384
    for tile in range(6):
        in_rows[tile] = arrived_ref[:, tile * LANES : (tile + 1) * LANES].astype(jnp.float32)
    for pair in range(6):
        gathered = []
        for mode in (2 * pair, 2 * pair + 1):
            pieces = []
            loaded = [
                jnp.concatenate(
                    [
                        in_rows.at[3 * turn + tile][pl.ds(2 * mode + part, sources, stride=step), :]
                        for tile in range(3)
                    ],
                    1,
                )
                for turn in range(2)
                for part in range(2)
            ]
            for group in range(4):
                for value in loaded:
                    if group:
                        value = pltpu.roll(value, wide - 96 * group, 1)
                    pieces.append(value[:, :LANES])
            gathered.append(jnp.concatenate(pieces).astype(jnp.bfloat16))
        spectrum = jnp.dot(
            forward_ref[...], jnp.concatenate(gathered, 1), preferred_element_type=jnp.float32
        ).astype(jnp.bfloat16)
        half = spectrum.shape[0] // 2
        filtered = []
        for side in range(2):
            mode = 2 * pair + side
            lanes = slice(side * LANES, (side + 1) * LANES)
            both = jnp.concatenate([spectrum[:half, lanes], spectrum[half:, lanes]], 1)
            layer = jnp.dot(both, first_ref[...], preferred_element_type=jnp.float32)
            layer = jnp.maximum(layer + first_shift_ref[...], 0.0).astype(jnp.bfloat16)
            layer = jnp.dot(layer, second_ref[...], preferred_element_type=jnp.float32)
            layer = layer + second_shift_ref[...]
            layer = layer - jnp.clip(layer, -shrink_level, shrink_level)
            layer = (layer * mask_ref[:, mode : mode + 1]).astype(jnp.bfloat16)
            filtered.append(jnp.concatenate([layer[:, :LANES], layer[:, LANES:]]))
        back = jnp.dot(
            inverse_ref[...], jnp.concatenate(filtered, 1), preferred_element_type=jnp.float32
        )
        for side in range(2):
            mode = 2 * pair + side
            for turn in range(2):
                for part in range(2):
                    total = None
                    for group in range(4):
                        first = ((group * 2 + turn) * 2 + part) * sources
                        piece = back[first : first + sources, side * LANES : (side + 1) * LANES]
                        piece = jnp.concatenate(
                            [piece, jnp.zeros((sources, wide - LANES), jnp.float32)], 1
                        )
                        if group:
                            piece = pltpu.roll(piece, 96 * group, 1)
                        total = piece if total is None else total + piece
                    total = total * factor_ref[mode]
                    for tile in range(3):
                        out_rows.at[3 * turn + tile][
                            pl.ds(2 * mode + part, sources, stride=step), :
                        ] = total[:, tile * LANES : (tile + 1) * LANES]
    for tile in range(6):
        out_ref[:, tile * LANES : (tile + 1) * LANES] = out_rows[tile].astype(jnp.bfloat16)


def inverse_kernel(modes_ref, tokens_ref, normed_ref, table_ref, out_ref, mixed_ref):
    block, rows, wide = 96, 192, 384
    filtered = jnp.dot(table_ref[...], modes_ref[...], preferred_element_type=jnp.float32)
    for turn in range(2):
        lanes = slice(turn * wide, (turn + 1) * wide)
        for source in range(8):
            place = slice(source * block, (source + 1) * block)
            mixed_ref[place, lanes] = (
                tokens_ref[source, turn, :block].astype(jnp.float32)
                + normed_ref[place, lanes].astype(jnp.float32)
                + filtered[place, lanes]
            ).astype(jnp.bfloat16)
        for group in range(4):
            first = turn * wide + group * block
            out_ref[2 * group + turn] = jnp.concatenate(
                [
                    mixed_ref[part * rows : (part + 1) * rows, first : first + block]
                    for part in range(4)
                ],
                1,
            )


def unpack_kernel(arrived_ref, gain_ref, bias_ref, out_ref, normed_ref):
    block, rows = 96, 192
    for part in range(4):
        place = slice(part * rows, (part + 1) * rows)
        row = jnp.concatenate(
            [arrived_ref[source, :, part * block : (part + 1) * block] for source in range(8)], 1
        )
        out_ref[place] = row
        values = row.astype(jnp.float32)
        center = jnp.mean(values, axis=-1, keepdims=True)
        spread = jnp.mean(jnp.square(values - center), axis=-1, keepdims=True)
        values = (values - center) * lax.rsqrt(spread + norm_epsilon)
        normed_ref[place] = (values * gain_ref[...] + bias_ref[...]).astype(jnp.bfloat16)


def local_call(body, outs, *operands, scratch=(), scalars=0, flops=0):
    specs = [pl.BlockSpec(memory_space=pltpu.VMEM)] * (len(operands) - scalars)
    specs += [pl.BlockSpec(memory_space=pltpu.SMEM)] * scalars
    moved = sum(item.size * item.dtype.itemsize for item in operands)
    return pl.pallas_call(
        body,
        out_shape=outs,
        in_specs=specs,
        out_specs=jax.tree.map(lambda _: pl.BlockSpec(memory_space=pltpu.VMEM), outs),
        scratch_shapes=list(scratch),
        cost_estimate=pl.CostEstimate(flops=flops, bytes_accessed=moved, transcendentals=0),
    )(*operands)


def fetch_half(weight, core):
    rows = weight.shape[0] // 2
    mine = lax.dynamic_slice_in_dim(weight, core * rows, rows, 0)
    return lax.ppermute(mine, "ch", [(0, 1), (1, 0)])


def join_halves(fetched, core):
    siblings = [(place, place ^ 1) for place in range(lax.axis_size("lat"))]
    shared = lax.ppermute(fetched, "lat", siblings)
    low = jnp.where(core == 0, fetched, shared)
    high = jnp.where(core == 0, shared, fetched)
    return jnp.concatenate([low, high])


def shards(
    grid_tokens,
    first_gain,
    first_bias,
    first_filter,
    first_shift,
    second_filter,
    second_shift,
    mode_mask,
    second_gain,
    second_bias,
    up_weight,
    up_bias,
    down_weight,
    down_bias,
):
    lat_count = lax.axis_size("lat")
    lon_count = lax.axis_size("lon")
    ch_count = lax.axis_size("ch")
    samples, rows_here, cols_here, channel_count = grid_tokens.shape
    full_width = cols_here * lon_count
    full_height = rows_here * lat_count
    part_chans = channel_count // ch_count
    mode_count = full_width // 2
    spread_count = lat_count * lon_count
    modes_here = mode_count // spread_count
    ch_place = lax.axis_index("ch")
    lat_place, lon_place = lax.axis_index("lat"), lax.axis_index("lon")
    core = lat_place % 2
    bf16 = jnp.bfloat16
    block = channel_count // lon_count
    wide = 4 * block
    plane = ("lat", "ch")
    plane_count = lat_count * ch_count
    plane_modes = mode_count // plane_count
    swap = [(0, 1), (1, 0)]

    by_row = grid_tokens.reshape(lon_count, ch_count, cols_here, channel_count)
    row_tokens = lax.dynamic_index_in_dim(by_row, ch_place, 1, keepdims=False)
    mask_rows = jnp.pad(
        mode_mask.T.astype(jnp.float32), ((0, 8 - modes_here), (0, wide - full_height))
    )
    send_shape = jax.ShapeDtypeStruct((lon_count, ch_count, cols_here + 16, wide), bf16)
    send = local_call(pack_kernel, send_shape, row_tokens, mask_rows)
    tokens = lax.all_to_all(send, "lon", split_axis=0, concat_axis=0, tiled=True)

    up_fetched = fetch_half(up_weight, core)
    biases = lax.ppermute(jnp.concatenate([up_bias, down_bias]), "ch", swap)
    hidden_here = up_bias.shape[0]
    up_bias_other, down_bias_other = biases[:hidden_here], biases[hidden_here:]
    blocks_here = first_filter.shape[1]
    owner = lon_place // blocks_here == ch_place
    at = lon_place % blocks_here

    def block_of(array):
        own = lax.dynamic_index_in_dim(array, at, 2, keepdims=False)
        return jnp.where(owner, own, lax.ppermute(own, "ch", swap))

    filters = block_of(jnp.stack([first_filter, second_filter]))
    shifts = block_of(jnp.stack([first_shift, second_shift]))
    shifts = jnp.pad(shifts, ((0, 0), (0, 0), (0, LANES - block))).reshape(2, 1, 2 * LANES)

    lon_forward = lon_table(full_width, mode_count)
    forward_rows = jnp.swapaxes(lon_forward, 0, 1).reshape(2 * mode_count, full_width)
    inverse_rows = forward_rows.T
    group, turn, source = jnp.meshgrid(
        jnp.arange(4), jnp.arange(2), jnp.arange(plane_count), indexing="ij"
    )
    row_order = rows_here * (source // ch_count) + ch_count * (2 * group + turn) + source % ch_count
    lat_forward = lat_table(full_height, row_order.reshape(-1).astype(jnp.int32))
    lat_inverse = lat_forward.T

    gain = lax.dynamic_slice_in_dim(first_gain, lon_place * block, block, 0)
    bias = lax.dynamic_slice_in_dim(first_bias, lon_place * block, block, 0)
    gain, bias = jnp.tile(gain, 4)[None], jnp.tile(bias, 4)[None]
    row_shape = jax.ShapeDtypeStruct((full_width, channel_count), bf16)
    transform_flops = 2 * full_width * full_width * channel_count

    def over_plane(array):
        moved = lax.all_to_all(
            array.reshape(plane_count, 2 * plane_modes, channel_count),
            plane,
            split_axis=0,
            concat_axis=0,
            tiled=True,
        )
        return moved.reshape(full_width, channel_count)

    normed, spectrum = local_call(
        forward_kernel,
        (row_shape, row_shape),
        tokens,
        gain,
        bias,
        forward_rows,
        flops=transform_flops,
    )
    spectrum, up_fetched = lax.optimization_barrier((spectrum, up_fetched))
    up_other = join_halves(up_fetched, core)
    arrived = over_plane(spectrum)

    masks = tokens[:, 0, cols_here + 8 : cols_here + 8 + modes_here, :full_height]
    mine = lax.dynamic_slice_in_dim(masks, ch_place * (lon_count // 2), lon_count // 2, 0)
    mask = mine.reshape(plane_modes, full_height).T.astype(jnp.float32)
    first_mode = (lat_place * ch_count + ch_place) * plane_modes
    factor = jnp.where(first_mode + jnp.arange(plane_modes) == 0, 1.0, 2.0)
    row_scratch = pltpu.VMEM((6, full_width, LANES), jnp.float32)
    back = local_call(
        modes_kernel,
        row_shape,
        arrived,
        lat_forward,
        lat_inverse,
        filter_matrix(filters[0]),
        shifts[0],
        filter_matrix(filters[1]),
        shifts[1],
        mask,
        factor,
        scratch=[row_scratch] * 2,
        scalars=1,
        flops=transform_flops,
    )
    modes = over_plane(back)
    packed = local_call(
        inverse_kernel,
        jax.ShapeDtypeStruct((lon_count, full_width // 4, wide), bf16),
        modes,
        tokens,
        normed,
        inverse_rows,
        scratch=[pltpu.VMEM((full_width, channel_count), bf16)],
        flops=transform_flops,
    )
    packed, down_ready = lax.optimization_barrier((packed, down_weight))
    down_other = join_halves(fetch_half(down_ready, core), core)
    row = lax.all_to_all(packed, "lon", split_axis=0, concat_axis=0, tiled=True)
    mixed, normed_two = local_call(
        unpack_kernel, (row_shape, row_shape), row, second_gain[None], second_bias[None]
    )
    bias_low = jnp.where(ch_place == 0, down_bias, down_bias_other)
    bias_high = jnp.where(ch_place == 0, down_bias_other, down_bias)
    down_shift = jnp.concatenate([bias_low, bias_high])
    total = mixed.astype(jnp.float32) + down_shift
    for up, up_shift, down in (
        (up_weight, up_bias, down_weight),
        (up_other, up_bias_other, down_other),
    ):
        hidden = jnp.dot(normed_two, up, preferred_element_type=jnp.float32) + up_shift
        hidden = (0.5 * hidden * (1.0 + lax.erf(hidden * math.sqrt(0.5)))).astype(bf16)
        partial = jnp.dot(hidden, down, preferred_element_type=jnp.float32).astype(bf16)
        total = total + partial.astype(jnp.float32)
    result = total.astype(bf16)
    low, high = result[:, :part_chans], result[:, part_chans:]
    kept = jnp.where(ch_place == 0, low, high)
    given = jnp.where(ch_place == 0, high, low)
    received = lax.ppermute(given, "ch", swap)
    even = jnp.where(ch_place == 0, kept, received)
    odd = jnp.where(ch_place == 0, received, kept)
    return jnp.stack([even, odd])[None]


def solution(mesh):
    in_specs = (
        P(None, "lat", "lon", None),
        P(),
        P(),
        P(None, "ch", None, None),
        P(None, "ch", None),
        P(None, "ch", None, None),
        P(None, "ch", None),
        P(None, ("lat", "lon")),
        P(),
        P(),
        P(None, "ch"),
        P("ch"),
        P("ch", None),
        P("ch"),
    )
    out_specs = P(None, ("lat", "lon"), None, "ch")
    return jax.shard_map(shards, mesh=mesh, in_specs=in_specs, out_specs=out_specs, check_vma=False)
```
